256 devices in a mesh: seq: 32 (over x, y, core), head: 8 (over z).
Axes of the slice: x: 4, y: 4, z: 8, core: 2. Of those that a mesh axis runs over, the one named last changes fastest.
Arguments:
- queries: float32 [65536, 1024], P('seq', 'head'), may hold values from -600 to 600
- keys: float32 [65536, 1024], P('seq', 'head'), may hold values from -6 to 6
- values: float32 [65536, 1024], P('seq', 'head'), may hold values from -6 to 6
- proj_e: float32 [65536, 256], P(('seq', 'head')), may hold values from -0.0234375 to 0.0234375
- proj_f: float32 [65536, 256], P(('seq', 'head')), may hold values from -0.0234375 to 0.0234375
- grad_out: float32 [65536, 1024], P('seq', 'head'), may hold values from -6 to 6
Outputs:
- grad_queries: float32 [65536, 1024], P('seq', 'head')
- grad_keys: float32 [65536, 1024], P('seq', 'head')
- grad_values: float32 [65536, 1024], P('seq', 'head')
- grad_e: float32 [65536, 256], P(('seq', 'head'))
- grad_f: float32 [65536, 256], P(('seq', 'head'))
The draws below stay inside these ranges and needn't reach their ends.
All inputs are finite; a program needn't handle non-finite values.
Results may differ from the reference program's by a relative error of at most 0.0003.
Values sent between devices are 32-bit elements; how exact they have to be, the bound alone decides.
No kernel may reach another device: no remote copies, remote signals or barrier semaphores. Data moves between devices by JAX's collectives and lax.ppermute only.
A program may use at most 64 MiB of HBM per device.

```python
import math
import jax
import jax.numpy as jnp
from jax import lax

H = 16
HD = 64
KP = 256
D = 1024
TOKENS = 65536


def draw_queries(key, part):
    first = jax.random.fold_in(key, 0)
    base = jnp.clip(jax.random.normal(first, (TOKENS, D), jnp.float32), -5.0, 5.0)
    return base


def block_scale(stream_key, shape, pieces, low, top_value):
    factor_of, own = 1.0, jax.random.fold_in(stream_key, 6)
    for axis_at, parts in pieces:
        draws = jnp.exp(jax.random.uniform(jax.random.fold_in(own, axis_at), (parts,), jnp.float32, low / len(pieces), top_value / len(pieces)))
        factor_of = factor_of * jnp.repeat(draws, shape[axis_at] // parts).reshape([-1 if axis == axis_at else 1 for axis in range(len(shape))])
    return factor_of


def gaussian(key, shape, scale, reach, shards=(), held_as=jnp.bfloat16):
    entries = scale * jax.random.normal(key, shape, jnp.float32)
    if shards:
        entries = entries * block_scale(key, shape, shards, -0.22, 0.18)
    return jnp.clip(entries, -reach, reach).astype(held_as)


def setup_inputs(seed: int = 0) -> dict:
    seeds = jax.random.split(jax.random.key(seed), 7)
    return {
        "queries": draw_queries(jax.random.fold_in(seeds[6], 71), 0),
        "keys": gaussian(seeds[1], (TOKENS, D), 1.0, 6.0, ((0, 32), (1, 8)), jnp.float32),
        "values": gaussian(seeds[2], (TOKENS, D), 1.0, 6.0, ((0, 32), (1, 8)), jnp.float32),
        "proj_e": gaussian(seeds[3], (TOKENS, KP), TOKENS ** -0.5, 0.0234375, ((0, 256),), jnp.float32),
        "proj_f": gaussian(seeds[4], (TOKENS, KP), TOKENS ** -0.5, 0.0234375, ((0, 256),), jnp.float32),
        "grad_out": gaussian(seeds[5], (TOKENS, D), 1.0, 6.0, ((0, 32), (1, 8)), jnp.float32),
    }


def reference(queries, keys, values, proj_e, proj_f, grad_out):
    highest = lax.Precision.HIGHEST
    scale = 1.0 / math.sqrt(HD)
    count = queries.shape[0]

    def split_heads(field):
        return field.reshape(count, H, HD).transpose(1, 0, 2)

    def one_head(carry, items):
        grad_e, grad_f = carry
        query, key_h, value_h, cotangent = items
        proj_keys = jnp.dot(proj_e.T, key_h, precision=highest)
        proj_vals = jnp.dot(proj_f.T, value_h, precision=highest)
        scores = jnp.dot(query, proj_keys.T, precision=highest) * scale
        scores = scores - lax.optimization_barrier(jnp.max(scores, axis=-1, keepdims=True))
        weights = jnp.exp(scores)
        probs = weights / lax.optimization_barrier(jnp.sum(weights, axis=-1, keepdims=True))
        attended = jnp.dot(probs, proj_vals, precision=highest)
        grad_probs = jnp.dot(cotangent, proj_vals.T, precision=highest)
        delta = lax.optimization_barrier(jnp.sum(cotangent * attended, axis=-1, keepdims=True))
        grad_scores = probs * (grad_probs - delta)
        grad_query = jnp.dot(grad_scores, proj_keys, precision=highest) * scale
        grad_pkeys = jnp.dot(grad_scores.T, query, precision=highest) * scale
        grad_pvals = jnp.dot(probs.T, cotangent, precision=highest)
        grad_key = jnp.dot(proj_e, grad_pkeys, precision=highest)
        grad_value = jnp.dot(proj_f, grad_pvals, precision=highest)
        grad_e = grad_e + jnp.dot(key_h, grad_pkeys.T, precision=highest)
        grad_f = grad_f + jnp.dot(value_h, grad_pvals.T, precision=highest)
        return ((grad_e, grad_f), (grad_query, grad_key, grad_value))
    start = (jnp.zeros(proj_e.shape, jnp.float32), jnp.zeros(proj_f.shape, jnp.float32))
    items = (split_heads(queries), split_heads(keys), split_heads(values), split_heads(grad_out))
    (grad_e, grad_f), (grad_q, grad_k, grad_v) = lax.scan(one_head, start, items)

    def join_heads(field):
        return field.transpose(1, 0, 2).reshape(count, H * HD)
    return (join_heads(grad_q), join_heads(grad_k), join_heads(grad_v), grad_e, grad_f)
```

```python
import math

import jax
import jax.numpy as jnp
from jax import lax
from jax.sharding import PartitionSpec as P

HD = 64

HIGHEST = lax.Precision.HIGHEST
HIGH = lax.Precision.HIGH


def seq_perm(move):
    pairs = []
    for x in range(4):
        for y in range(4):
            for core in range(2):
                tx, ty, tc = move(x, y, core)
                pairs.append(((x * 4 + y) * 2 + core, ((tx % 4) * 4 + ty % 4) * 2 + tc))
    return pairs


CORE = seq_perm(lambda x, y, c: (x, y, 1 - c))
X = [seq_perm(lambda x, y, c, k=k: (x + k, y, c)) for k in range(4)]
Y = [seq_perm(lambda x, y, c, k=k: (x, y + k, c)) for k in range(4)]


def sum_over_seq(first, second):
    even = lax.axis_index("seq") % 2 == 0
    mine = jnp.where(even, first, second)
    mine = mine + lax.ppermute(jnp.where(even, second, first), "seq", CORE)
    for ring in (X, Y):
        one, two, three = (lax.ppermute(mine, "seq", ring[k]) for k in (1, 2, 3))
        mine = (mine + two) + (one + three)
    other = lax.ppermute(mine, "seq", CORE)
    return jnp.where(even, mine, other), jnp.where(even, other, mine)


def rings(n):
    up = [(i, (i + 1) % n) for i in range(n)]
    down = [(i, (i - 1) % n) for i in range(n)]
    return up, down


def gather_blocks(own, n):
    up, down = rings(n)
    half = n // 2
    rows = own.shape[0] // 2
    blocks = [None] * n
    blocks[0] = own
    above = below = own
    for step in range(1, half):
        above = lax.ppermute(above, "head", down)
        below = lax.ppermute(below, "head", up)
        blocks[step] = above
        blocks[n - step] = below
    top = lax.ppermute(above[:rows], "head", down)
    bottom = lax.ppermute(below[rows:], "head", up)
    blocks[half] = jnp.concatenate([top, bottom], axis=0)
    return blocks


def scatter_blocks(terms, n):
    up, down = rings(n)
    half = n // 2
    rows = terms[0].shape[0] // 2
    rising = lax.ppermute(terms[half][:rows], "head", up)
    falling = lax.ppermute(terms[half][rows:], "head", down)
    rising = terms[half - 1] + jnp.concatenate([rising, jnp.zeros_like(rising)], axis=0)
    falling = terms[n - half + 1] + jnp.concatenate([jnp.zeros_like(falling), falling], axis=0)
    for step in range(half - 1, 0, -1):
        rising = lax.ppermute(rising, "head", up)
        falling = lax.ppermute(falling, "head", down)
        if step > 1:
            rising = rising + terms[step - 1]
            falling = falling + terms[n - step + 1]
    return terms[0] + rising + falling


def rotate(array, shift):
    rows = array.shape[0]
    return lax.dynamic_slice_in_dim(jnp.concatenate([array, array], axis=0), shift, rows, axis=0)


def on_device(queries, keys, values, proj_e, proj_f, grad_out):
    scale = 1.0 / math.sqrt(HD)
    count, width = queries.shape
    heads = width // HD
    block, depth = proj_e.shape
    n = count // block
    z = lax.axis_index("head")
    keys_r = rotate(keys, z * block)
    values_r = rotate(values, z * block)
    e_blocks = gather_blocks(proj_e, n)
    f_blocks = gather_blocks(proj_f, n)
    key_part = sum(
        jnp.einsum("tk,tc->kc", e_blocks[d], keys_r[d * block : (d + 1) * block], precision=HIGHEST)
        for d in range(n)
    )
    val_part = sum(
        jnp.einsum("tk,tc->kc", f_blocks[d], values_r[d * block : (d + 1) * block], precision=HIGH)
        for d in range(n)
    )
    proj_keys, proj_vals = sum_over_seq(key_part, val_part)
    query3 = queries.reshape(count, heads, HD)
    cotan3 = grad_out.reshape(count, heads, HD)
    pkeys3 = proj_keys.reshape(depth, heads, HD)
    pvals3 = proj_vals.reshape(depth, heads, HD)
    scores = jnp.einsum("thd,khd->htk", query3, pkeys3, precision=HIGHEST) * scale
    scores = scores - jnp.max(scores, axis=-1, keepdims=True)
    weights = jnp.exp(scores)
    probs = weights / jnp.sum(weights, axis=-1, keepdims=True)
    grad_probs = jnp.einsum("thd,khd->htk", cotan3, pvals3, precision=HIGH)
    delta = jnp.sum(probs * grad_probs, axis=-1, keepdims=True)
    grad_scores = probs * (grad_probs - delta)
    grad_query = jnp.einsum("htk,khd->thd", grad_scores, pkeys3, precision=HIGH) * scale
    gkeys_part = jnp.einsum("htk,thd->khd", grad_scores, query3, precision=HIGH) * scale
    gvals_part = jnp.einsum("htk,thd->khd", probs, cotan3, precision=HIGH)
    grad_pkeys, grad_pvals = sum_over_seq(
        gkeys_part.reshape(depth, width), gvals_part.reshape(depth, width)
    )
    term_e = jnp.einsum("tc,kc->tk", keys_r, grad_pkeys, precision=HIGH)
    term_f = jnp.einsum("tc,kc->tk", values_r, grad_pvals, precision=HIGH)
    grad_e = scatter_blocks([term_e[d * block : (d + 1) * block] for d in range(n)], n)
    grad_f = scatter_blocks([term_f[d * block : (d + 1) * block] for d in range(n)], n)
    full_e = jnp.concatenate(e_blocks, axis=0)
    full_f = jnp.concatenate(f_blocks, axis=0)
    grad_key = jnp.dot(full_e, grad_pkeys, precision=HIGH)
    grad_value = jnp.dot(full_f, grad_pvals, precision=HIGH)
    back = (n - z) % n * block
    return (
        grad_query.reshape(count, width),
        rotate(grad_key, back),
        rotate(grad_value, back),
        grad_e,
        grad_f,
    )


def solution(mesh):
    tokens = P("seq", "head")
    rows = P(("seq", "head"), None)
    return jax.shard_map(
        on_device,
        mesh=mesh,
        in_specs=(tokens, tokens, tokens, rows, rows, tokens),
        out_specs=(tokens, tokens, tokens, rows, rows),
        check_vma=False,
    )
```

```python
import functools
import math

import jax
import jax.numpy as jnp
from jax import lax
from jax.experimental import pallas as pl
from jax.experimental.pallas import tpu as pltpu
from jax.sharding import PartitionSpec as P


HD = 64

F32 = jnp.float32
BF16 = jnp.bfloat16


def seq_perm(move):
    pairs = []
    for x in range(4):
        for y in range(4):
            for core in range(2):
                tx, ty, tc = move(x, y, core)
                pairs.append(((x * 4 + y) * 2 + core, ((tx % 4) * 4 + ty % 4) * 2 + tc))
    return pairs


CORE = seq_perm(lambda x, y, c: (x, y, 1 - c))


FIRST = [seq_perm(lambda x, y, c, k=k: (x, y + k, c) if c else (x + k, y, c)) for k in range(4)]
SECOND = [seq_perm(lambda x, y, c, k=k: (x + k, y, c) if c else (x, y + k, c)) for k in range(4)]


def sum_over_seq(first, second):
    even = lax.axis_index("seq") % 2 == 0
    mine = jnp.where(even, first, second)
    mine = mine + lax.ppermute(jnp.where(even, second, first), "seq", CORE)
    for ring in (FIRST, SECOND):
        one, two, three = (lax.ppermute(mine, "seq", ring[k]) for k in (1, 2, 3))
        mine = (mine + two) + (one + three)
    other = lax.ppermute(mine, "seq", CORE)
    return jnp.where(even, mine, other), jnp.where(even, other, mine)


def shift(x, perm):
    return lax.ppermute(x, "head", perm)


def rings(n):
    up = [(i, (i + 1) % n) for i in range(n)]
    down = [(i, (i - 1) % n) for i in range(n)]
    return up, down


def gather_blocks(own, other, n):
    up, down = rings(n)
    half = n // 2
    e, f = [own] + [None] * (n - 1), [other] + [None] * (n - 1)
    for step in range(1, half):
        e[step] = shift(e[step - 1], down)
        e[-step] = shift(e[(1 - step) % n], up)
        f[step] = shift(f[step - 1], down)
        f[-step] = shift(f[(1 - step) % n], up)
    e[half] = shift(e[half - 1], down)
    f[half] = shift(f[half + 1], up)
    return e, f


def scatter_blocks(terms_e, terms_f, n, beside):
    up, down = rings(n)
    half = n // 2
    e_up = shift(terms_e[half], up)
    f_down = shift(terms_f[half], down)
    e_down = shift(terms_e[half + 1], down)
    f_up = shift(terms_f[half - 1], up)
    done = []
    for step in range(2, half + 1):
        near, far = half + 1 - step, half - 1 + step
        e_up = shift(e_up + terms_e[near], up)
        f_down = shift(f_down + terms_f[far], down)
        if step < half:
            e_down = e_down + terms_e[far + 1]
            f_up = f_up + terms_f[near - 1]
            work = beside[len(done)]()
            f_up, work = lax.optimization_barrier((f_up, work))
            done.append(work)
            e_down = shift(e_down, down)
            f_up = shift(f_up, up)
    grad_e = (terms_e[0] + e_down) + e_up
    grad_f = (terms_f[0] + f_up) + f_down
    return grad_e, grad_f, done


def two(x):
    high = x.astype(BF16)
    return high, (x - high.astype(F32)).astype(BF16)


def three(x):
    high = x.astype(BF16)
    rest = x - high.astype(F32)
    mid = rest.astype(BF16)
    return high, mid, (rest - mid.astype(F32)).astype(BF16)


def move(to, source):
    rows = 32

    def step(i, carry):
        at = pl.ds(pl.multiple_of(i * rows, rows), rows)
        to[at, :] = source[at, :]
        return carry

    lax.fori_loop(0, source.shape[0] // rows, step, 0)


def mm(a, b):
    return lax.dot_general(a, b, (((1,), (0,)), ((), ())), preferred_element_type=F32)


VMEM = pl.BlockSpec(memory_space=pltpu.VMEM)
SMEM = pl.BlockSpec(memory_space=pltpu.SMEM)
LIMIT = 16 * 1024 * 1024


def call(body, out, n_in, scratch=(), flops=0, moved=0):
    single = not isinstance(out, tuple)
    return pl.pallas_call(
        body,
        out_shape=out,
        in_specs=[SMEM] + [VMEM] * n_in,
        out_specs=VMEM if single else tuple(VMEM for _ in out),
        scratch_shapes=list(scratch),
        compiler_params=pltpu.CompilerParams(vmem_limit_bytes=LIMIT),
        cost_estimate=pl.CostEstimate(flops=flops, bytes_accessed=moved, transcendentals=0),
    )


def six_pass(left_t, right):
    rows = left_t.shape[0]
    l1, l2, l3 = three(left_t)
    r1, r2, r3 = three(right)
    a = mm(jnp.concatenate([l1, l2, l3], axis=0), r1)
    b = mm(jnp.concatenate([l1, l2], axis=0), r2)
    c = mm(l1, r3)
    small = (a[2 * rows :] + b[rows:]) + c
    return (small + (a[rows : 2 * rows] + b[:rows])) + a[:rows]


def three_pass(left_t, right):
    rows = left_t.shape[0]
    l1, l2 = two(left_t)
    r1, r2 = two(right)
    a = mm(jnp.concatenate([l1, l2], axis=0), r1)
    return (a[rows:] + mm(l1, r2)) + a[:rows]


def partial_body(n, distances, z_ref, *refs):
    count = len(distances)
    es, fs = refs[:count], refs[count : 2 * count]
    keys, values = refs[2 * count : 2 * count + 2]
    pk_ref, pv_ref, e_stack, f_stack, e_buf, f_buf, came, went = refs[-8:]
    block = e_buf.shape[1]
    for j in range(count):
        pltpu.make_async_copy(es[j], e_buf.at[j], came.at[0, j]).start()
        pltpu.make_async_copy(fs[j], f_buf.at[j], came.at[1, j]).start()
    if len(refs) > 2 * count + 10:
        pk_ref[...] = refs[2 * count + 2][...]
        pv_ref[...] = refs[2 * count + 3][...]
    else:
        pk_ref[...] = jnp.zeros_like(pk_ref)
        pv_ref[...] = jnp.zeros_like(pv_ref)

    def out(i):
        d = jnp.int32(distances[0])
        for j, distance in enumerate(distances):
            d = jnp.where(i == j, distance, d)
        rows = pl.ds(pl.multiple_of(d * block, block), block)
        return d, (
            pltpu.make_async_copy(e_buf.at[i], e_stack.at[rows], went.at[0, i]),
            pltpu.make_async_copy(f_buf.at[i], f_stack.at[rows], went.at[1, i]),
        )

    def step(i, carry):
        d, copies = out(i)
        start = pl.multiple_of(lax.rem(z_ref[0] + d, n) * block, block)
        pltpu.make_async_copy(es[0], e_buf.at[i], came.at[0, i]).wait()
        pltpu.make_async_copy(fs[0], f_buf.at[i], came.at[1, i]).wait()
        for copy in copies:
            copy.start()
        pk_ref[...] += six_pass(keys[pl.ds(start, block), :].T, e_buf[i])
        pv_ref[...] += three_pass(values[pl.ds(start, block), :].T, f_buf[i])
        return carry

    lax.fori_loop(0, count, step, 0)

    def finish(i, carry):
        for copy in out(i)[1]:
            copy.wait()
        return carry

    lax.fori_loop(0, count, finish, 0)


def partial(n, z, distances, es, fs, keys, values, before=()):
    block, depth = es[0].shape
    width = keys.shape[1]
    count = len(distances)
    small = jax.ShapeDtypeStruct((width, depth), F32)
    stack = pltpu.HBM((n * block, depth), F32)
    anywhere = pl.BlockSpec(memory_space=pl.ANY)
    buffers = pltpu.VMEM((count, block, depth), F32)
    sems = pltpu.SemaphoreType.DMA((2, count))
    first = 2 * count + 3
    blocks = [
        which[d] if count == 1 else pltpu.with_memory_space_constraint(which[d], pltpu.HBM)
        for which in (es, fs)
        for d in distances
    ]
    return pl.pallas_call(
        functools.partial(partial_body, n, distances),
        out_shape=(small, small, stack, stack),
        in_specs=[SMEM] + [anywhere] * (2 * count) + [VMEM] * 2
        + ([VMEM, VMEM, anywhere, anywhere] if before else []),
        out_specs=(VMEM, VMEM, anywhere, anywhere),
        scratch_shapes=[buffers, buffers, sems, sems],
        input_output_aliases={first + 2: 2, first + 3: 3} if before else {},
        compiler_params=pltpu.CompilerParams(vmem_limit_bytes=LIMIT),
        cost_estimate=pl.CostEstimate(
            flops=10**8 * count, bytes_accessed=2**20 * count, transcendentals=0
        ),
    )(z, *blocks, keys, values, *before)


def middle_body(scale, q_ref, g_ref, pk_ref, pv_ref, gq_ref, gpk_ref, gpv_ref, ws, wt, wg, wq):
    heads = 2
    tile = q_ref.shape[0]
    width, depth = pk_ref.shape

    @pl.when(pl.program_id(0) == 0)
    def _():
        row = lax.broadcasted_iota(jnp.int32, (width, depth), 0)
        for h in range(heads):
            rows = slice(h * HD, (h + 1) * HD)
            p1, p2, p3 = three(pk_ref[rows, :])
            ws[h] = jnp.concatenate([p1, p2, p1, p1], axis=0)
            wt[h] = jnp.concatenate([p3, p2], axis=0)
            v1, v2 = two(pv_ref[rows, :])
            wg[h] = jnp.concatenate([v1, v2, v1, jnp.zeros_like(v1)], axis=0)
            own = (row >= h * HD) & (row < (h + 1) * HD)
            t1, t2 = two(jnp.where(own, pk_ref[...], 0.0).T)
            wq[h] = jnp.concatenate([t1, t2], axis=1)
        gpk_ref[...] = jnp.zeros_like(gpk_ref)
        gpv_ref[...] = jnp.zeros_like(gpv_ref)

    q = q_ref[...] * scale
    g = g_ref[...]
    qt1, qt2 = two(q.T)
    gt1, gt2 = two(g.T)
    left = lax.broadcasted_iota(jnp.int32, (tile, width), 1) < HD
    q_turned, g_turned = pltpu.roll(q, HD, 1), pltpu.roll(g, HD, 1)

    def doubled(x, turned, h):
        return jnp.where(left, turned, x) if h else jnp.where(left, x, turned)

    def products(h):
        x = doubled(q, q_turned, h)
        x1 = x.astype(BF16)
        rest = x - x1.astype(F32)
        last = rest - rest.astype(BF16).astype(F32)
        x23 = jnp.where(left, rest, last).astype(BF16)
        x12 = jnp.where(left, x, rest).astype(BF16)
        scores = mm(x12, wt[h]) + mm(jnp.concatenate([x1, x23], axis=1), ws[h])
        y = doubled(g, g_turned, h)
        y1 = y.astype(BF16)
        y2 = (y - y1.astype(F32)).astype(BF16)
        return scores, mm(jnp.concatenate([y1, y2], axis=1), wg[h])

    def softmax(scores, grad_probs):
        weights = jnp.exp(scores - jnp.max(scores, axis=-1, keepdims=True))
        inverse = 1.0 / jnp.sum(weights, axis=-1, keepdims=True)
        delta = jnp.sum(weights * grad_probs, axis=-1, keepdims=True) * inverse
        probs = weights * inverse
        return two(probs), two(probs * (grad_probs - delta))

    def gradients(h, probs, grad_scores):
        rows = slice(h * HD, (h + 1) * HD)
        p1, p2 = probs
        d1, d2 = grad_scores
        a = mm(jnp.concatenate([gt1[rows], gt2[rows]], axis=0), p1)
        gpv_ref[rows, :] += (a[HD:] + mm(gt1[rows], p2)) + a[:HD]
        a = mm(jnp.concatenate([qt1[rows], qt2[rows]], axis=0), d1)
        gpk_ref[rows, :] += (a[HD:] + mm(qt1[rows], d2)) + a[:HD]
        a = mm(d1, wq[h])
        return (a[:, width:] + mm(d2, wq[h, :, :width])) + a[:, :width]

    both = [products(h) for h in range(heads)]
    gq_ref[...] = sum(gradients(h, *softmax(*both[h])) for h in range(heads)) * scale


def middle(queries, grad_out, pk, pv, scale):
    count, width = queries.shape
    depth = pk.shape[1]
    tile = 512
    rows = pl.BlockSpec((tile, width), lambda i: (i, 0))
    whole = pl.BlockSpec((width, depth), lambda i: (0, 0))
    small = jax.ShapeDtypeStruct((width, depth), F32)
    return pl.pallas_call(
        functools.partial(middle_body, scale),
        grid=(count // tile,),
        out_shape=(jax.ShapeDtypeStruct((count, width), F32), small, small),
        in_specs=[rows, rows, whole, whole],
        out_specs=(rows, whole, whole),
        scratch_shapes=[
            pltpu.VMEM((2, 2 * width, depth), BF16),
            pltpu.VMEM((2, width, depth), BF16),
            pltpu.VMEM((2, 2 * width, depth), BF16),
            pltpu.VMEM((2, depth, 2 * width), BF16),
        ],
        compiler_params=pltpu.CompilerParams(
            vmem_limit_bytes=LIMIT, dimension_semantics=("arbitrary",)
        ),
        cost_estimate=pl.CostEstimate(flops=10**10, bytes_accessed=2**22, transcendentals=2**20),
        name="middle",
    )(queries, grad_out, pk, pv)


def term_of(rows, weights):
    r1, r2 = two(rows)
    w1, w2 = two(weights)
    both = mm(jnp.concatenate([r1, r2], axis=1), jnp.concatenate([w1, w1], axis=0))
    return mm(r1, w2) + both


def terms_body(n, e_at, f_at, z_ref, keys, values, gpk, gpv, *refs):
    *outs, e_now, f_now = refs
    block = outs[0].shape[0]
    count = len(e_at)

    def step(i, carry):
        e_d, f_d = jnp.int32(0), jnp.int32(0)
        for j in range(count):
            e_d = jnp.where(i == j, e_at[j], e_d)
            f_d = jnp.where(i == j, f_at[j], f_d)
        e_start = pl.multiple_of(lax.rem(z_ref[0] + e_d, n) * block, block)
        f_start = pl.multiple_of(lax.rem(z_ref[0] + f_d, n) * block, block)
        e_now[...] = term_of(keys[pl.ds(e_start, block), :], gpk[...])
        f_now[...] = term_of(values[pl.ds(f_start, block), :], gpv[...])
        for j in range(count):
            @pl.when(i == j)
            def _():
                move(outs[j], e_now)
                move(outs[count + j], f_now)
        return carry

    lax.fori_loop(0, count, step, 0)


def grads_body(z_ref, rows_ref, grads_ref, out_ref):
    width = grads_ref.shape[0]
    w1, w2 = two(grads_ref[...].T)
    r1, r2 = two(rows_ref[...])
    a = mm(r1, jnp.concatenate([w1, w2], axis=1))
    out_ref[...] = (a[:, width:] + mm(r2, w1)) + a[:, :width]


def products_of(z, stack, grads, n):
    width, depth = grads.shape
    block = stack.shape[0] // n
    return pl.pallas_call(
        grads_body,
        out_shape=jax.ShapeDtypeStruct((stack.shape[0], width), F32),
        grid_spec=pltpu.PrefetchScalarGridSpec(
            num_scalar_prefetch=1,
            grid=(n,),
            in_specs=[
                pl.BlockSpec((block, depth), lambda d, z_ref: (d, 0)),
                pl.BlockSpec((width, depth), lambda d, z_ref: (0, 0)),
            ],
            out_specs=pl.BlockSpec((block, width), lambda d, z_ref: (lax.rem(z_ref[0] + d, n), 0)),
        ),
        compiler_params=pltpu.CompilerParams(
            vmem_limit_bytes=LIMIT, dimension_semantics=("arbitrary",)
        ),
        cost_estimate=pl.CostEstimate(flops=10**9, bytes_accessed=2**22, transcendentals=0),
    )(z, stack, grads)


def whole(queries, keys, values, proj_e, proj_f, grad_out):
    scale = 1.0 / math.sqrt(HD)
    count, _ = queries.shape
    block, depth = proj_e.shape
    n = count // block
    z = lax.axis_index("head").astype(jnp.int32).reshape(1)
    square = jax.ShapeDtypeStruct((block, depth), F32)
    half = n // 2

    def run(body, out, *operands, scratch=(), flops=10**9):
        kernel = call(functools.partial(body, n), out, len(operands), scratch, flops, 2**22)
        return kernel(z, *operands)

    es, fs = gather_blocks(proj_e, proj_f, n)
    sums = ()
    for distances in (
        [d for d in range(n) if min(d, n - d) < half - 1], [half - 1, half + 1], [half]
    ):
        sums = partial(n, z, distances, es, fs, keys, values, sums)
    pk, pv, e_stack, f_stack = sums
    proj_keys, proj_vals = sum_over_seq(pk, pv)
    grad_query, gpk, gpv = middle(queries, grad_out, proj_keys, proj_vals, scale)
    gpk, gpv = sum_over_seq(gpk, gpv)
    terms_e, terms_f = [None] * n, [None] * n
    for e_at, f_at in (
        ([half, half + 1], [half, half - 1]),
        (
            [d for d in range(n) if d not in (half, half + 1)],
            [d for d in range(n) if d not in (half, half - 1)],
        ),
    ):
        blocks = run(
            lambda n, *refs, at=(e_at, f_at): terms_body(n, *at, *refs),
            (square,) * (len(e_at) + len(f_at)), keys, values, gpk, gpv,
            scratch=[pltpu.VMEM((block, depth), F32)] * 2,
        )
        for i, d in enumerate(e_at):
            terms_e[d] = blocks[i]
        for i, d in enumerate(f_at):
            terms_f[d] = blocks[len(e_at) + i]
    grad_e, grad_f, (grad_key, grad_value) = scatter_blocks(
        terms_e, terms_f, n,
        [lambda: products_of(z, e_stack, gpk, n), lambda: products_of(z, f_stack, gpv, n)],
    )
    return grad_query, grad_key, grad_value, grad_e, grad_f


def solution(mesh):
    tokens = P("seq", "head")
    rows = P(("seq", "head"), None)
    return jax.shard_map(
        whole,
        mesh=mesh,
        in_specs=(tokens, tokens, tokens, rows, rows, tokens),
        out_specs=(tokens, tokens, tokens, rows, rows),
        check_vma=False,
    )
```

```python
import functools
import math

import jax
import jax.numpy as jnp
from jax import lax
from jax.experimental import pallas as pl
from jax.experimental.pallas import tpu as pltpu
from jax.sharding import PartitionSpec as P


HD = 64

F32 = jnp.float32
BF16 = jnp.bfloat16


def seq_perm(move):
    pairs = []
    for x in range(4):
        for y in range(4):
            for core in range(2):
                tx, ty, tc = move(x, y, core)
                pairs.append(((x * 4 + y) * 2 + core, ((tx % 4) * 4 + ty % 4) * 2 + tc))
    return pairs


CORE = seq_perm(lambda x, y, c: (x, y, 1 - c))


FIRST = [seq_perm(lambda x, y, c, k=k: (x, y + k, c) if c else (x + k, y, c)) for k in range(4)]
SECOND = [seq_perm(lambda x, y, c, k=k: (x + k, y, c) if c else (x, y + k, c)) for k in range(4)]


def sum_over_seq(first, second):
    even = lax.axis_index("seq") % 2 == 0
    mine = jnp.where(even, first, second)
    mine = mine + lax.ppermute(jnp.where(even, second, first), "seq", CORE)
    for ring in (FIRST, SECOND):
        one, two, three = (lax.ppermute(mine, "seq", ring[k]) for k in (1, 2, 3))
        mine = (mine + two) + (one + three)
    other = lax.ppermute(mine, "seq", CORE)
    return jnp.where(even, mine, other), jnp.where(even, other, mine)


def shift(x, perm):
    return lax.ppermute(x, "head", perm)


def rings(n):
    up = [(i, (i + 1) % n) for i in range(n)]
    down = [(i, (i - 1) % n) for i in range(n)]
    return up, down


def gather_blocks(own, other, n):
    up, down = rings(n)
    half = n // 2
    e, f = [own] + [None] * (n - 1), [other] + [None] * (n - 1)
    for step in range(1, half):
        e[step] = shift(e[step - 1], down)
        e[-step] = shift(e[(1 - step) % n], up)
        f[step] = shift(f[step - 1], down)
        f[-step] = shift(f[(1 - step) % n], up)
    e[half] = shift(e[half - 1], down)
    f[half] = shift(f[half + 1], up)
    return e, f


def scatter_blocks(terms_e, terms_f, n, beside):
    up, down = rings(n)
    half = n // 2
    e_up = shift(terms_e[half], up)
    f_down = shift(terms_f[half], down)
    e_down = shift(terms_e[half + 1], down)
    f_up = shift(terms_f[half - 1], up)
    done = []
    for step in range(2, half + 1):
        near, far = half + 1 - step, half - 1 + step
        e_up = shift(e_up + terms_e[near], up)
        f_down = shift(f_down + terms_f[far], down)
        if step < half:
            e_down = e_down + terms_e[far + 1]
            f_up = f_up + terms_f[near - 1]
            work = beside[len(done)]()
            f_up, work = lax.optimization_barrier((f_up, work))
            done.append(work)
            e_down = shift(e_down, down)
            f_up = shift(f_up, up)
    return (terms_e[0], e_down, e_up), (terms_f[0], f_up, f_down), done


def two(x):
    high = x.astype(BF16)
    return high, (x - high.astype(F32)).astype(BF16)


def three(x):
    high = x.astype(BF16)
    rest = x - high.astype(F32)
    mid = rest.astype(BF16)
    return high, mid, (rest - mid.astype(F32)).astype(BF16)


def move(to, source):
    rows = 32

    def step(i, carry):
        at = pl.ds(pl.multiple_of(i * rows, rows), rows)
        to[at, :] = source[at, :]
        return carry

    lax.fori_loop(0, source.shape[0] // rows, step, 0)


def mm(a, b):
    return lax.dot_general(a, b, (((1,), (0,)), ((), ())), preferred_element_type=F32)


VMEM = pl.BlockSpec(memory_space=pltpu.VMEM)
SMEM = pl.BlockSpec(memory_space=pltpu.SMEM)
LIMIT = 16 * 1024 * 1024


def call(body, out, n_in, scratch=(), flops=0, moved=0):
    single = not isinstance(out, tuple)
    return pl.pallas_call(
        body,
        out_shape=out,
        in_specs=[SMEM] + [VMEM] * n_in,
        out_specs=VMEM if single else tuple(VMEM for _ in out),
        scratch_shapes=list(scratch),
        compiler_params=pltpu.CompilerParams(vmem_limit_bytes=LIMIT),
        cost_estimate=pl.CostEstimate(flops=flops, bytes_accessed=moved, transcendentals=0),
    )


def six_pass(left_t, right):
    rows = left_t.shape[0]
    l1, l2, l3 = three(left_t)
    r1, r2, r3 = three(right)
    a = mm(jnp.concatenate([l1, l2, l3], axis=0), r1)
    b = mm(jnp.concatenate([l1, l2], axis=0), r2)
    c = mm(l1, r3)
    small = (a[2 * rows :] + b[rows:]) + c
    return (small + (a[rows : 2 * rows] + b[:rows])) + a[:rows]


def three_pass(left_t, right):
    rows = left_t.shape[0]
    l1, l2 = two(left_t)
    r1, r2 = two(right)
    a = mm(jnp.concatenate([l1, l2], axis=0), r1)
    return (a[rows:] + mm(l1, r2)) + a[:rows]


def partial_body(n, distances, z_ref, *refs):
    count = len(distances)
    es, fs = refs[:count], refs[count : 2 * count]
    keys, values = refs[2 * count : 2 * count + 2]
    pk_ref, pv_ref, e_stack, f_stack, e_buf, f_buf, came, went = refs[-8:]
    block = e_buf.shape[1]
    for j in range(count):
        pltpu.make_async_copy(es[j], e_buf.at[j], came.at[0, j]).start()
        pltpu.make_async_copy(fs[j], f_buf.at[j], came.at[1, j]).start()
    if len(refs) > 2 * count + 10:
        pk_ref[...] = refs[2 * count + 2][...]
        pv_ref[...] = refs[2 * count + 3][...]
    else:
        pk_ref[...] = jnp.zeros_like(pk_ref)
        pv_ref[...] = jnp.zeros_like(pv_ref)

    def out(i):
        d = jnp.int32(distances[0])
        for j, distance in enumerate(distances):
            d = jnp.where(i == j, distance, d)
        rows = pl.ds(pl.multiple_of(d * block, block), block)
        return d, (
            pltpu.make_async_copy(e_buf.at[i], e_stack.at[rows], went.at[0, i]),
            pltpu.make_async_copy(f_buf.at[i], f_stack.at[rows], went.at[1, i]),
        )

    def step(i, carry):
        d, copies = out(i)
        start = pl.multiple_of(lax.rem(z_ref[0] + d, n) * block, block)
        pltpu.make_async_copy(es[0], e_buf.at[i], came.at[0, i]).wait()
        pltpu.make_async_copy(fs[0], f_buf.at[i], came.at[1, i]).wait()
        for copy in copies:
            copy.start()
        pk_ref[...] += six_pass(keys[pl.ds(start, block), :].T, e_buf[i])
        pv_ref[...] += three_pass(values[pl.ds(start, block), :].T, f_buf[i])
        return carry

    lax.fori_loop(0, count, step, 0)

    def finish(i, carry):
        for copy in out(i)[1]:
            copy.wait()
        return carry

    lax.fori_loop(0, count, finish, 0)


def partial(n, z, distances, es, fs, keys, values, before=()):
    block, depth = es[0].shape
    width = keys.shape[1]
    count = len(distances)
    small = jax.ShapeDtypeStruct((width, depth), F32)
    stack = pltpu.HBM((n * block, depth), F32)
    anywhere = pl.BlockSpec(memory_space=pl.ANY)
    buffers = pltpu.VMEM((count, block, depth), F32)
    sems = pltpu.SemaphoreType.DMA((2, count))
    first = 2 * count + 3
    blocks = [
        which[d] if count == 1 else pltpu.with_memory_space_constraint(which[d], pltpu.HBM)
        for which in (es, fs)
        for d in distances
    ]
    return pl.pallas_call(
        functools.partial(partial_body, n, distances),
        out_shape=(small, small, stack, stack),
        in_specs=[SMEM] + [anywhere] * (2 * count) + [VMEM] * 2
        + ([VMEM, VMEM, anywhere, anywhere] if before else []),
        out_specs=(VMEM, VMEM, anywhere, anywhere),
        scratch_shapes=[buffers, buffers, sems, sems],
        input_output_aliases={first + 2: 2, first + 3: 3} if before else {},
        compiler_params=pltpu.CompilerParams(vmem_limit_bytes=LIMIT),
        cost_estimate=pl.CostEstimate(
            flops=10**8 * count, bytes_accessed=2**20 * count, transcendentals=0
        ),
    )(z, *blocks, keys, values, *before)


def middle_body(scale, q_ref, g_ref, pk_ref, pv_ref, gq_ref, gpk_ref, gpv_ref, ws, wt, wg, wq):
    heads = 2
    tile = q_ref.shape[0]
    width, depth = pk_ref.shape

    @pl.when(pl.program_id(0) == 0)
    def _():
        row = lax.broadcasted_iota(jnp.int32, (width, depth), 0)
        for h in range(heads):
            rows = slice(h * HD, (h + 1) * HD)
            p1, p2, p3 = three(pk_ref[rows, :])
            ws[h] = jnp.concatenate([p1, p2, p1, p1], axis=0)
            wt[h] = jnp.concatenate([p3, p2], axis=0)
            v1, v2 = two(pv_ref[rows, :])
            wg[h] = jnp.concatenate([v1, v2, v1, jnp.zeros_like(v1)], axis=0)
            own = (row >= h * HD) & (row < (h + 1) * HD)
            t1, t2 = two(jnp.where(own, pk_ref[...], 0.0).T)
            wq[h] = jnp.concatenate([t1, t2], axis=1)
        gpk_ref[...] = jnp.zeros_like(gpk_ref)
        gpv_ref[...] = jnp.zeros_like(gpv_ref)

    q = q_ref[...] * scale
    g = g_ref[...]
    qt1, qt2 = two(q.T)
    gt1, gt2 = two(g.T)
    left = lax.broadcasted_iota(jnp.int32, (tile, width), 1) < HD
    q_turned, g_turned = pltpu.roll(q, HD, 1), pltpu.roll(g, HD, 1)

    def doubled(x, turned, h):
        return jnp.where(left, turned, x) if h else jnp.where(left, x, turned)

    def products(h):
        x = doubled(q, q_turned, h)
        x1 = x.astype(BF16)
        rest = x - x1.astype(F32)
        last = rest - rest.astype(BF16).astype(F32)
        x23 = jnp.where(left, rest, last).astype(BF16)
        x12 = jnp.where(left, x, rest).astype(BF16)
        scores = mm(x12, wt[h]) + mm(jnp.concatenate([x1, x23], axis=1), ws[h])
        y = doubled(g, g_turned, h)
        y1 = y.astype(BF16)
        y2 = (y - y1.astype(F32)).astype(BF16)
        return scores, mm(jnp.concatenate([y1, y2], axis=1), wg[h])

    def softmax(scores, grad_probs):
        weights = jnp.exp(scores - jnp.max(scores, axis=-1, keepdims=True))
        inverse = 1.0 / jnp.sum(weights, axis=-1, keepdims=True)
        delta = jnp.sum(weights * grad_probs, axis=-1, keepdims=True) * inverse
        probs = weights * inverse
        return two(probs), two(probs * (grad_probs - delta))

    def gradients(h, probs, grad_scores):
        rows = slice(h * HD, (h + 1) * HD)
        p1, p2 = probs
        d1, d2 = grad_scores
        a = mm(jnp.concatenate([gt1[rows], gt2[rows]], axis=0), p1)
        gpv_ref[rows, :] += (a[HD:] + mm(gt1[rows], p2)) + a[:HD]
        a = mm(jnp.concatenate([qt1[rows], qt2[rows]], axis=0), d1)
        gpk_ref[rows, :] += (a[HD:] + mm(qt1[rows], d2)) + a[:HD]
        a = mm(d1, wq[h])
        return (a[:, width:] + mm(d2, wq[h, :, :width])) + a[:, :width]

    both = [products(h) for h in range(heads)]
    gq_ref[...] = sum(gradients(h, *softmax(*both[h])) for h in range(heads)) * scale


def middle(queries, grad_out, pk, pv, scale):
    count, width = queries.shape
    depth = pk.shape[1]
    tile = 512
    rows = pl.BlockSpec((tile, width), lambda i: (i, 0))
    whole = pl.BlockSpec((width, depth), lambda i: (0, 0))
    small = jax.ShapeDtypeStruct((width, depth), F32)
    return pl.pallas_call(
        functools.partial(middle_body, scale),
        grid=(count // tile,),
        out_shape=(jax.ShapeDtypeStruct((count, width), F32), small, small),
        in_specs=[rows, rows, whole, whole],
        out_specs=(rows, whole, whole),
        scratch_shapes=[
            pltpu.VMEM((2, 2 * width, depth), BF16),
            pltpu.VMEM((2, width, depth), BF16),
            pltpu.VMEM((2, 2 * width, depth), BF16),
            pltpu.VMEM((2, depth, 2 * width), BF16),
        ],
        compiler_params=pltpu.CompilerParams(
            vmem_limit_bytes=LIMIT, dimension_semantics=("arbitrary",)
        ),
        cost_estimate=pl.CostEstimate(flops=10**10, bytes_accessed=2**22, transcendentals=2**20),
        name="middle",
    )(queries, grad_out, pk, pv)


def term_of(rows, weights):
    r1, r2 = two(rows)
    w1, w2 = two(weights)
    both = mm(jnp.concatenate([r1, r2], axis=1), jnp.concatenate([w1, w1], axis=0))
    return mm(r1, w2) + both


def terms_body(n, e_at, f_at, z_ref, keys, values, gpk, gpv, *refs):
    *outs, e_now, f_now = refs
    block = outs[0].shape[0]
    count = len(e_at)
    if count == 2:
        for at, rows, grads, to in (
            (e_at, keys, gpk, outs[:count]),
            (f_at, values, gpv, outs[count:]),
        ):
            for d, ref in zip(at, to):
                start = pl.multiple_of(lax.rem(z_ref[0] + d, n) * block, block)
                ref[...] = term_of(rows[pl.ds(start, block), :], grads[...])
        return

    def step(i, carry):
        e_d, f_d = jnp.int32(0), jnp.int32(0)
        for j in range(count):
            e_d = jnp.where(i == j, e_at[j], e_d)
            f_d = jnp.where(i == j, f_at[j], f_d)
        e_start = pl.multiple_of(lax.rem(z_ref[0] + e_d, n) * block, block)
        f_start = pl.multiple_of(lax.rem(z_ref[0] + f_d, n) * block, block)
        e_now[...] = term_of(keys[pl.ds(e_start, block), :], gpk[...])
        f_now[...] = term_of(values[pl.ds(f_start, block), :], gpv[...])
        for j in range(count):
            @pl.when(i == j)
            def _():
                move(outs[j], e_now)
                move(outs[count + j], f_now)
        return carry

    lax.fori_loop(0, count, step, 0)


def grads_body(z_ref, rows_ref, grads_ref, out_ref):
    width = grads_ref.shape[0]
    w1, w2 = two(grads_ref[...].T)
    r1, r2 = two(rows_ref[...])
    a = mm(r1, jnp.concatenate([w1, w2], axis=1))
    out_ref[...] = (a[:, width:] + mm(r2, w1)) + a[:, :width]


def products_of(z, stack, grads, n):
    width, depth = grads.shape
    block = stack.shape[0] // n
    return pl.pallas_call(
        grads_body,
        out_shape=jax.ShapeDtypeStruct((stack.shape[0], width), F32),
        grid_spec=pltpu.PrefetchScalarGridSpec(
            num_scalar_prefetch=1,
            grid=(n,),
            in_specs=[
                pl.BlockSpec((block, depth), lambda d, z_ref: (d, 0)),
                pl.BlockSpec((width, depth), lambda d, z_ref: (0, 0)),
            ],
            out_specs=pl.BlockSpec((block, width), lambda d, z_ref: (lax.rem(z_ref[0] + d, n), 0)),
        ),
        compiler_params=pltpu.CompilerParams(
            vmem_limit_bytes=LIMIT, dimension_semantics=("arbitrary",)
        ),
        cost_estimate=pl.CostEstimate(flops=10**9, bytes_accessed=2**22, transcendentals=0),
    )(z, stack, grads)


def add_body(a, b, c, d, e, f, out_ref, other_ref):
    rows = 64

    def step(i, carry):
        at = pl.ds(pl.multiple_of(i * rows, rows), rows)
        out_ref[at, :] = (a[at, :] + b[at, :]) + c[at, :]
        other_ref[at, :] = (d[at, :] + e[at, :]) + f[at, :]
        return carry

    lax.fori_loop(0, out_ref.shape[0] // rows, step, 0)


def add_both(first, second):
    square = jax.ShapeDtypeStruct(first[0].shape, F32)
    return pl.pallas_call(
        add_body,
        out_shape=(square, square),
        in_specs=[VMEM] * 6,
        out_specs=(VMEM, VMEM),
        compiler_params=pltpu.CompilerParams(vmem_limit_bytes=LIMIT),
        cost_estimate=pl.CostEstimate(flops=2**18, bytes_accessed=2**21, transcendentals=0),
        name="add_both",
    )(*first, *second)


def whole(queries, keys, values, proj_e, proj_f, grad_out):
    scale = 1.0 / math.sqrt(HD)
    count, _ = queries.shape
    block, depth = proj_e.shape
    n = count // block
    z = lax.axis_index("head").astype(jnp.int32).reshape(1)
    square = jax.ShapeDtypeStruct((block, depth), F32)
    half = n // 2

    def run(body, out, *operands, scratch=(), flops=10**9):
        kernel = call(functools.partial(body, n), out, len(operands), scratch, flops, 2**22)
        return kernel(z, *operands)

    es, fs = gather_blocks(proj_e, proj_f, n)
    sums = ()
    for distances in (
        [d for d in range(n) if min(d, n - d) < half - 1], [half - 1, half + 1], [half]
    ):
        sums = partial(n, z, distances, es, fs, keys, values, sums)
    pk, pv, e_stack, f_stack = sums
    proj_keys, proj_vals = sum_over_seq(pk, pv)
    grad_query, gpk, gpv = middle(queries, grad_out, proj_keys, proj_vals, scale)
    gpk, gpv = sum_over_seq(gpk, gpv)
    terms_e, terms_f = [None] * n, [None] * n
    for e_at, f_at in (
        ([half, half + 1], [half, half - 1]),
        (
            [d for d in range(n) if d not in (half, half + 1)],
            [d for d in range(n) if d not in (half, half - 1)],
        ),
    ):
        blocks = run(
            lambda n, *refs, at=(e_at, f_at): terms_body(n, *at, *refs),
            (square,) * (len(e_at) + len(f_at)), keys, values, gpk, gpv,
            scratch=[pltpu.VMEM((block, depth), F32)] * 2,
        )
        for i, d in enumerate(e_at):
            terms_e[d] = blocks[i]
        for i, d in enumerate(f_at):
            terms_f[d] = blocks[len(e_at) + i]
    parts_e, parts_f, (grad_key, grad_value) = scatter_blocks(
        terms_e, terms_f, n,
        [lambda: products_of(z, e_stack, gpk, n), lambda: products_of(z, f_stack, gpv, n)],
    )
    grad_e, grad_f = add_both(parts_e, parts_f)
    return grad_query, grad_key, grad_value, grad_e, grad_f


def solution(mesh):
    tokens = P("seq", "head")
    rows = P(("seq", "head"), None)
    return jax.shard_map(
        whole,
        mesh=mesh,
        in_specs=(tokens, tokens, tokens, rows, rows, tokens),
        out_specs=(tokens, tokens, tokens, rows, rows),
        check_vma=False,
    )
```
